32 devices in a mesh: comp: 2 (over core), face: 4 (over y, x), tile: 4 (over z).
Axes of the slice: x: 2, y: 2, z: 4, core: 2. Of those that a mesh axis runs over, the one named last changes fastest.
Arguments:
- tokens: bfloat16 [2, 256, 64, 512], P('comp', 'tile', 'face'), may hold values from -6 to 6
- norm_gains: bfloat16 [2, 3, 512], P('comp'), may hold values from 0.5 to 1.5
- qkv_weight: bfloat16 [2, 512, 1536], P('comp'), may hold values from -0.25 to 0.25
- out_weight: bfloat16 [2, 512, 512], P('comp'), may hold values from -0.25 to 0.25
- cross_query: bfloat16 [2, 512, 512], P('comp'), may hold values from -0.25 to 0.25
- cross_kv: bfloat16 [2, 512, 1024], P('comp'), may hold values from -0.25 to 0.25
- cross_out: bfloat16 [2, 512, 512], P('comp'), may hold values from -0.25 to 0.25
- up_weight: bfloat16 [2, 512, 2048], P('comp'), may hold values from -0.25 to 0.25
- down_weight: bfloat16 [2, 2048, 512], P('comp'), may hold values from -0.125 to 0.125
- intersection_list: int32 [2, 32, 4, 4], P(None, 'tile', 'face'), may hold values from 0 to 7, all different within a row
- land_bands: int32 [4, 4], replicated, may hold values from 0 to 7
Outputs:
- evolved: bfloat16 [2, 256, 64, 512], P('comp', 'tile', 'face')
The draws below stay inside these ranges and needn't reach their ends.
Inputs may be any that keep to these rules, and one draw needn't show every extreme that they name: `intersection_list`: each band names 4 different bands of the other component's tile. `land_bands`: the land bands of an ocean tile are its first ones.
All inputs are finite; a program needn't handle non-finite values.
Results may differ from the reference program's by a relative error of at most 0.0045.
Values may be sent and summed in bfloat16 or wider, within the bound.
A program may use at most 128 MiB of HBM per device.

```python
import jax
import jax.numpy as jnp
from jax import lax

D = 512
FF = 2048
HEADS = 8
RX = 16
BR = 8
NB = 8
KC = 4
RY = 64
NLAT = 256
NLON = 64
N_FACE = 4
N_TILE = 4


def set_ends(result, own_key, least, largest):
    dims = result.shape
    index_at = [jax.random.randint(jax.random.fold_in(own_key, axis), (), 0, dims[axis]) for axis in range(len(dims))]
    result = result.at[tuple(index_at)].set(least)
    longest = dims.index(max(dims))
    index_at[longest] = (index_at[longest] + 1) % dims[longest]
    return result.at[tuple(index_at)].set(largest)


def block_levels(stream_key, shape, cuts, smallest, largest):
    level = 1.0
    for position, parts in cuts:
        draws = jax.random.uniform(jax.random.fold_in(jax.random.fold_in(stream_key, 6), position), (parts,), jnp.float32, smallest / len(cuts), largest / len(cuts))
        level = level * jnp.repeat(jnp.exp(draws), shape[position] // parts).reshape((-1,) + (1,) * (len(shape) - 1 - position))
    return level


def distinct(stream_key, rows, count, top, lift):
    order = jax.random.permutation(jax.random.fold_in(stream_key, 1), count)
    favour = order
    for power in range(3):
        favour = favour * favour // count
    favour = favour * lift // count
    lots = jax.random.randint(jax.random.fold_in(stream_key, 2), (rows, count), 0, 4096) + favour
    fixed_rows = jax.random.permutation(jax.random.fold_in(stream_key, 3), rows)[jnp.arange(count) % rows]
    lots = jnp.where(jnp.arange(rows)[:, None] == fixed_rows[None, :], 1 << 14, lots)
    score = lots * count + jnp.arange(count)
    return lax.top_k(score.astype(jnp.int32), top)[1].astype(jnp.int32)


def noise(own_key, shape, scale, limit, split=(), held_as=jnp.bfloat16):
    drawn = jax.random.normal(own_key, shape, jnp.float32) * scale
    if len(split) > 0:
        drawn = block_levels(own_key, shape, split, -0.22, 0.18) * drawn
    return jnp.clip(drawn, min=-limit, max=limit).astype(held_as)


def setup_inputs(seed: int = 0) -> dict:
    key_of = jax.random.split(jax.random.key(seed), 12)
    tokens = noise(key_of[0], (2, NLAT, NLON, D), 1.0, 6.0, ((0, 2), (1, 4), (2, 4)))
    norm_gains = jnp.clip(1.0 + 0.1 * jax.random.normal(key_of[1], (2, 3, D), jnp.float32), 0.5, 1.5).astype(jnp.bfloat16)
    qkv_weight = noise(key_of[2], (2, D, 3 * D), D ** -0.5, 0.25, ((0, 2),))
    out_weight = noise(key_of[3], (2, D, D), D ** -0.5, 0.25, ((0, 2),))
    cross_query = noise(key_of[4], (2, D, D), D ** -0.5, 0.25, ((0, 2),))
    cross_kv = noise(key_of[5], (2, D, 2 * D), D ** -0.5, 0.25, ((0, 2),))
    cross_out = noise(key_of[6], (2, D, D), D ** -0.5, 0.25, ((0, 2),))
    up_weight = noise(key_of[7], (2, D, FF), D ** -0.5, 0.25, ((0, 2),))
    down_weight = noise(key_of[8], (2, FF, D), FF ** -0.5, 0.125, ((0, 2),))
    intersection_list = distinct(key_of[9], 2 * (NB * N_TILE) * N_FACE, NB, KC, 0).reshape((2, NB * N_TILE, N_FACE, KC))
    land_bands = set_ends(jax.random.randint(key_of[10], (N_TILE, N_FACE), 0, NB), jax.random.fold_in(key_of[10], 1), 0, NB - 1).astype(jnp.int32)
    return {"tokens": tokens, "norm_gains": norm_gains, "qkv_weight": qkv_weight, "out_weight": out_weight, "cross_query": cross_query, "cross_kv": cross_kv, "cross_out": cross_out, "up_weight": up_weight, "down_weight": down_weight, "intersection_list": intersection_list, "land_bands": land_bands}


EPSILON = 1e-05

def norm_round(values, gain):
    mean_square = lax.optimization_barrier(jnp.mean(values * values, axis=-1, keepdims=True))
    return (values * lax.rsqrt(mean_square + EPSILON) * gain.astype(jnp.float32)).astype(jnp.bfloat16)

def attend(queries, key_rows, value_rows, usable):
    blocks, count_q, feat_width = queries.shape
    count_k = key_rows.shape[1]
    head_dim = feat_width // HEADS
    score_scale = head_dim ** (-0.5)
    q_heads = queries.astype(jnp.float32).reshape(blocks, count_q, HEADS, head_dim)
    k_heads = key_rows.astype(jnp.float32).reshape(blocks, count_k, HEADS, head_dim)
    v_heads = value_rows.astype(jnp.float32).reshape(blocks, count_k, HEADS, head_dim)
    scores = jnp.einsum('bqhd,bkhd->bhqk', q_heads, k_heads) * score_scale
    scores = jnp.where(usable[:, None, None, :], scores, -1e+30)
    highest = jnp.maximum(lax.optimization_barrier(jnp.max(scores, axis=-1, keepdims=True)), 0.0)
    exp_terms = jnp.exp(scores - highest)
    denominator = lax.optimization_barrier(jnp.sum(exp_terms, axis=-1, keepdims=True)) + jnp.exp(-highest)
    weights = (exp_terms / denominator).astype(jnp.bfloat16)
    blended = jnp.einsum('bhqk,bkhd->bqhd', weights.astype(jnp.float32), v_heads)
    return blended.reshape(blocks, count_q, feat_width).astype(jnp.bfloat16)

def window_bands(array_in):
    grouped = array_in.reshape((NB + 2, BR) + array_in.shape[1:])
    joined = jnp.concatenate([grouped[0:NB], grouped[1:NB + 1], grouped[2:NB + 2]], axis=1)
    return joined.reshape((NB, -1) + array_in.shape[2:])

def to_blocks(grid):
    last_dim = grid.shape[-1]
    pieces = grid.reshape(N_TILE, NB, BR, N_FACE, RX, last_dim)
    return pieces.transpose(0, 3, 1, 2, 4, 5).reshape(N_TILE * N_FACE, NB, BR * RX, last_dim)

def from_blocks(blocked):
    last_dim = blocked.shape[-1]
    pieces = blocked.reshape(N_TILE, N_FACE, NB, BR, RX, last_dim)
    return pieces.transpose(0, 2, 3, 1, 4, 5).reshape(NLAT, NLON, last_dim)

def reference(tokens, norm_gains, qkv_weight, out_weight, cross_query, cross_kv, cross_out, up_weight, down_weight, intersection_list, land_bands):
    land_flat = land_bands.reshape(N_TILE * N_FACE)
    grid_rows = jnp.arange(NLAT, dtype=jnp.int32)
    grid_cols = jnp.arange(NLON, dtype=jnp.int32)
    land_grid = land_bands[grid_rows // RY][:, grid_cols // RX]
    sea_live = (grid_rows % RY // BR)[:, None] >= land_grid
    rows_pad = jnp.arange(NLAT + 2 * BR, dtype=jnp.int32) - BR
    lat_ok = (rows_pad >= 0) & (rows_pad < NLAT)
    rows_in = jnp.clip(rows_pad, 0, NLAT - 1)
    cols_pad = (jnp.arange(NLON + 2 * BR, dtype=jnp.int32) - BR) % NLON
    land_pad = land_bands[rows_in // RY][:, cols_pad // RX]
    sea_pad = (rows_in % RY // BR)[:, None] >= land_pad
    residuals = []
    window_parts = []
    cross_queries = []
    cross_pairs = []
    for component in range(2):
        residual_in = tokens[component].astype(jnp.float32)
        attn_input = norm_round(residual_in, norm_gains[component, 0]).reshape(NLAT * NLON, D)
        cross_input = norm_round(residual_in, norm_gains[component, 1]).reshape(NLAT * NLON, D)
        projected = jnp.dot(attn_input, qkv_weight[component], preferred_element_type=jnp.float32).astype(jnp.bfloat16).reshape(NLAT, NLON, 3 * D)
        pair_rows = projected[:, :, D:]
        pair_rows = jnp.concatenate([pair_rows[:, NLON - BR:], pair_rows, pair_rows[:, :BR]], axis=1)
        pair_rows = jnp.pad(pair_rows, ((BR, BR), (0, 0), (0, 0)))
        if component == 1:
            usable = lat_ok[:, None] & sea_pad
        else:
            usable = lat_ok[:, None] & jnp.ones_like(sea_pad)
        queries = projected[:, :, :D]

        def tile_window(tile_pos):
            tile_row = tile_pos // N_FACE
            tile_col = tile_pos % N_FACE
            row_start = (tile_row * RY).astype(jnp.int32)
            col_start = (tile_col * RX).astype(jnp.int32)
            zero_start = (tile_row * 0).astype(jnp.int32)
            pair_tile = lax.dynamic_slice(pair_rows, (row_start, col_start, zero_start), (RY + 2 * BR, RX + 2 * BR, 2 * D))
            usable_tile = lax.dynamic_slice(usable, (row_start, col_start), (RY + 2 * BR, RX + 2 * BR))
            query_tile = lax.dynamic_slice(queries, (row_start, col_start, zero_start), (RY, RX, D))
            pair_win = window_bands(pair_tile)
            return attend(query_tile.reshape(NB, BR * RX, D), pair_win[:, :, :D], pair_win[:, :, D:], window_bands(usable_tile))
        window_out = lax.map(tile_window, jnp.arange(N_TILE * N_FACE, dtype=jnp.int32))
        window_parts.append(from_blocks(window_out).reshape(NLAT * NLON, D))
        cq_grid = jnp.dot(cross_input, cross_query[component], preferred_element_type=jnp.float32).astype(jnp.bfloat16)
        ckv_grid = jnp.dot(cross_input, cross_kv[component], preferred_element_type=jnp.float32).astype(jnp.bfloat16)
        cross_queries.append(to_blocks(cq_grid.reshape(NLAT, NLON, D)))
        cross_pairs.append(to_blocks(ckv_grid.reshape(NLAT, NLON, 2 * D)))
        residuals.append(residual_in.reshape(NLAT * NLON, D))
    results = []
    for component in range(2):
        partner = 1 - component
        link_table = intersection_list[component].reshape(N_TILE, NB, N_FACE, KC).transpose(0, 2, 1, 3).reshape(N_TILE * N_FACE, NB, KC)
        partner_pairs = cross_pairs[partner]
        own_queries = cross_queries[component]

        def tile_cross(tile_pos):
            chosen = link_table[tile_pos]
            picked = jnp.take(partner_pairs[tile_pos], chosen, axis=0).reshape(NB, KC * BR * RX, 2 * D)
            key_floor = land_flat[tile_pos] * partner
            usable_keys = jnp.repeat(chosen >= key_floor, BR * RX, axis=1)
            return attend(own_queries[tile_pos], picked[:, :, :D], picked[:, :, D:], usable_keys)
        cross_res = from_blocks(lax.map(tile_cross, jnp.arange(N_TILE * N_FACE, dtype=jnp.int32))).reshape(NLAT * NLON, D)
        if component == 1:
            live_mask = jnp.where(sea_live, jnp.float32(1.0), jnp.float32(0.0)).reshape(NLAT * NLON, 1)
        else:
            live_mask = jnp.ones((NLAT * NLON, 1), jnp.float32)
        update = jnp.dot(window_parts[component], out_weight[component], preferred_element_type=jnp.float32)
        update = update + jnp.dot(cross_res, cross_out[component], preferred_element_type=jnp.float32)
        middle = residuals[component] + live_mask * update
        mlp_input = norm_round(middle, norm_gains[component, 2])
        hidden = jax.nn.silu(jnp.dot(mlp_input, up_weight[component], preferred_element_type=jnp.float32)).astype(jnp.bfloat16)
        result_rows = middle + live_mask * jnp.dot(hidden, down_weight[component], preferred_element_type=jnp.float32)
        results.append(result_rows.astype(jnp.bfloat16).reshape(NLAT, NLON, D))
    return jnp.stack(results)
```

```python
import functools

import jax
import jax.numpy as jnp
from jax import lax
from jax.experimental import pallas as pl
from jax.experimental.pallas import tpu as pltpu
from jax.sharding import PartitionSpec as P

HEADS = 8
BR = 8
KC = 4
EPSILON = 1e-05
EXTRA = 16
LOG2E = 1.4426950408889634
MESH = pl.DeviceIdType.MESH
F32 = jnp.float32
BF16 = jnp.bfloat16


def dot(a, b):
    return lax.dot_general(a, b, (((1,), (0,)), ((), ())), preferred_element_type=F32)


def dot_t(a, b):
    return lax.dot_general(a, b, (((1,), (1,)), ((), ())), preferred_element_type=F32)


def attend_bands(start, end, pairs, pair, keys_of, values_of, queries, scores, terms, peaks, result=None, held=None):
    cells = queries.shape[2] // 2
    half = pair // 2

    def score(b, p, slot):
        q = queries[b, p]
        top = jnp.zeros((8, 2 * cells), F32)
        if result is not None and held is not None:
            top = held[2][b, p]
        row = 0
        for keys in keys_of(b, p):
            rows = keys.shape[0]
            s = dot_t(keys, q)
            scores[slot][pl.ds(row, rows), :] = s
            top = jnp.maximum(top, jnp.max(s.reshape(rows // 8, 8, 2 * cells), axis=0))
            row += rows
        peaks[slot][...] = jnp.broadcast_to(jnp.max(top, axis=0, keepdims=True), (8, 2 * cells))

    def blend(b, p, slot):
        blended = dot(values_of(b, p), terms[slot][...])
        first, second = blended[:half, :cells], blended[half:pair, cells:]
        total = blended[pair : pair + 8, :]
        if result is None:
            held[0][b, p, :, pl.ds(0, cells)] = first
            held[0][b, p, :, pl.ds(cells, cells)] = second
            held[1][b, p] = total
            return
        total = total[0:1, :] + peaks[2 + slot][0:1, :]
        if held is not None:
            fade = peaks[4 + slot][0:1, :]
            total = total + held[1][b, p, 0:1, :] * fade
            first = first + held[0][b, p, :, pl.ds(0, cells)] * fade[:, :cells]
            second = second + held[0][b, p, :, pl.ds(cells, cells)] * fade[:, cells:]
        inverse = 1.0 / total
        first = first * inverse[:, :cells]
        second = second * inverse[:, cells:]
        result[b, :, pl.ds(p * pair, pair)] = jnp.concatenate([first, second], axis=0).T.astype(BF16)

    def weigh(b, p, slot):
        peak = peaks[slot][0:1, :]
        terms[slot][...] = jnp.exp2(scores[slot][...] - peak).astype(BF16)
        if result is None:
            held[2][b, p] = peaks[slot][...]
            return
        peaks[2 + slot][...] = jnp.exp2(-peaks[slot][...])
        if held is not None:
            peaks[4 + slot][...] = jnp.exp2(held[2][b, p] - peaks[slot][...])

    last = (pairs - 1) % 2
    terms[last][...] = jnp.zeros(terms[last].shape, BF16)
    peaks[2 + last][...] = jnp.ones(peaks[2 + last].shape, F32)
    peaks[4 + last][...] = jnp.ones(peaks[4 + last].shape, F32)
    score(start, 0, 0)

    @pl.loop(start, end)
    def _(b):
        for p in range(pairs):
            slot = p % 2
            if p + 1 < pairs:
                score(b, p + 1, 1 - slot)
            else:
                score(jnp.minimum(b + 1, end - 1), 0, 1 - slot)
            if p > 0:
                blend(b, p - 1, 1 - slot)
            else:
                blend(jnp.maximum(b - 1, start), pairs - 1, 1 - slot)
            weigh(b, p, slot)

    blend(end - 1, pairs - 1, last)


def kernel(
    links,
    land,
    tok5,
    tok4,
    gains_hbm,
    wqkv_hbm,
    wout_hbm,
    wcq_hbm,
    wckv_hbm,
    wcout_hbm,
    wup_hbm,
    wdown_hbm,
    out_ref,
    own,
    side,
    ends,
    part,
    gains,
    gains_p,
    wqkv,
    wout,
    wcq,
    wckv,
    wcout,
    wup,
    wdown,
    wv_t,
    qbd,
    cqbd,
    kwin,
    vwin,
    kcross,
    vcross,
    win_res,
    cross_res,
    cs0,
    cs1,
    ce0,
    ce1,
    ws0,
    ws1,
    we0,
    we1,
    m0,
    m1,
    m2,
    m3,
    m4,
    m5,
    held_values,
    held_totals,
    held_peaks,
    send_sem,
    recv_sem,
    local_sem,
):
    nb, groups, _, d = own.shape
    cells = groups * BR
    pair = 2 * (d // HEADS)
    pairs = d // pair
    vrows = pair + EXTRA
    comp, face, tile = (lax.axis_index(a) for a in ("comp", "face", "tile"))
    n_face, n_tile = lax.axis_size("face"), lax.axis_size("tile")
    left, right = lax.rem(face + n_face - 1, n_face), lax.rem(face + 1, n_face)
    up, down = lax.rem(tile + n_tile - 1, n_tile), lax.rem(tile + 1, n_tile)
    other = 1 - comp

    local = [
        pltpu.make_async_copy(src, dst, local_sem.at[i])
        for i, (src, dst) in enumerate(
            (
                (tok4, own),
                (gains_hbm, gains),
                (wqkv_hbm, wqkv),
                (wcq_hbm, wcq),
                (wcout_hbm, wcout),
                (wout_hbm, wout),
                (wup_hbm, wup),
                (wdown_hbm, wdown),
            )
        )
    ]
    for copy in local[:4]:
        copy.start()

    barrier = pltpu.get_barrier_semaphore()
    for target in ({"comp": other}, {"face": left}, {"face": right}, {"tile": up}, {"tile": down}):
        pl.semaphore_signal(barrier, inc=1, device_id=target, device_id_type=MESH)
    pl.semaphore_wait(barrier, 5)

    def remote(i, src, dst, target):
        return pltpu.make_async_remote_copy(
            src_ref=src,
            dst_ref=dst,
            send_sem=send_sem.at[i],
            recv_sem=recv_sem.at[i],
            device_id=target,
            device_id_type=MESH,
        )

    def to_face(i, first, count):
        bands = pl.ds(first, count)
        return [
            remote(i, tok5.at[bands, :, 0], side.at[pl.ds(1 + first, count), pl.ds(BR, BR)], {"face": left}),
            remote(i + 1, tok5.at[bands, :, 1], side.at[pl.ds(1 + first, count), pl.ds(0, BR)], {"face": right}),
        ]

    edge_copies = to_face(0, 0, 1) + to_face(2, nb - 1, 1)
    step = nb // 2
    near_copies = to_face(4, 1, step // 2)
    mid_copies = to_face(15, 1 + step // 2, step - step // 2)
    far_copies = to_face(13, 1 + step, nb - 2 - step)
    end_copies = [
        remote(6, tok4.at[0], ends.at[1], {"tile": up}),
        remote(7, tok4.at[nb - 1], ends.at[0], {"tile": down}),
    ]
    comp_copies = [
        remote(9, wckv_hbm, wckv, {"comp": other}),
        remote(8, tok4, part, {"comp": other}),
        remote(10, gains_hbm, gains_p, {"comp": other}),
    ]
    corner_copies = [
        remote(11, side.at[1], side.at[nb + 1], {"tile": up}),
        remote(12, side.at[nb], side.at[0], {"tile": down}),
    ]
    for copy in edge_copies + comp_copies + end_copies + near_copies + mid_copies + far_copies:
        copy.start()
    for copy in local[4:]:
        copy.start()

    is_air = comp == 0
    own_land = land[tile, face]

    def flag(cond):
        return jnp.where(cond, 1.0, 0.0).astype(F32)

    def usable(tile_at, face_at, band):
        return flag(is_air | (band >= land[tile_at, face_at]))

    def scaled(x):
        mean_square = jnp.mean(x * x, axis=-1, keepdims=True)
        return x * lax.rsqrt(mean_square + EPSILON)

    def expand(flags, counts, axis):
        shape = (sum(counts), 1) if axis == 0 else (1, sum(counts))
        at = lax.broadcasted_iota(jnp.int32, shape, axis)
        mask = jnp.full(shape, flags[0], F32)
        start = 0
        for value, count in zip(flags[1:], counts[:-1]):
            start += count
            mask = jnp.where(at >= start, value, mask)
        return mask

    def put_values(ref, at, lanes, vals, mask_row):
        width = vals.shape[1]
        extra = jnp.broadcast_to(mask_row, (EXTRA, width)).astype(BF16)
        for p in range(pairs):
            ref[at, pl.ds(p * vrows, pair), lanes] = vals[p * pair : (p + 1) * pair, :]
            ref[at, pl.ds(p * vrows + pair, EXTRA), lanes] = extra

    def put_queries(ref, b, q):
        lane = lax.broadcasted_iota(jnp.int32, (1, d), 1)
        low = lax.rem(lane, pair) < pair // 2
        q = q * float((d // HEADS) ** -0.5 * LOG2E)
        q_low = jnp.where(low, q, 0.0).astype(BF16)
        q_high = jnp.where(low, 0.0, q).astype(BF16)
        for p in range(pairs):
            ref[b, p, pl.ds(0, cells)] = q_low[:, p * pair : (p + 1) * pair]
            ref[b, p, pl.ds(cells, cells)] = q_high[:, p * pair : (p + 1) * pair]

    for copy in local[:4]:
        copy.wait()
    wv_t[0] = wqkv[:, 2 * d : 3 * d].T
    chunk = step * cells

    @pl.loop(0, nb // step)
    def _(c):
        base = c * step
        x = own[pl.ds(base, step)].astype(F32).reshape(chunk, d)
        x = scaled(x)
        flags = [usable(tile, face, base + j) for j in range(step)]
        xa = (x * gains[0:1, :].astype(F32) * expand(flags, [cells] * step, 0)).astype(BF16)
        xc = (x * gains[1:2, :].astype(F32)).astype(BF16)
        q = dot(xa, wqkv[:, 0:d])
        cq = dot(xc, wcq[...])
        k = dot(xa, wqkv[:, d : 2 * d]).astype(BF16)
        v = dot_t(wv_t[0], xa).astype(BF16)
        for j in range(step):
            rows = slice(j * cells, (j + 1) * cells)
            put_queries(qbd, base + j, q[rows])
            put_queries(cqbd, base + j, cq[rows])
            kwin[1 + base + j, pl.ds(0, cells)] = k[rows]
            put_values(vwin, 1 + base + j, pl.ds(0, cells), v[:, rows], jnp.full((1, cells), flags[j], F32))

    for copy in comp_copies:
        copy.wait_recv()
    wv_t[1] = wckv[:, d : 2 * d].T

    @pl.loop(0, nb // step)
    def _(c):
        base = c * step
        x = scaled(part[pl.ds(base, step)].astype(F32).reshape(chunk, d))
        flags = [flag((comp == 1) | (base + j >= own_land)) for j in range(step)]
        xp = (x * gains_p[1:2, :].astype(F32) * expand(flags, [cells] * step, 0)).astype(BF16)
        k = dot(xp, wckv[:, 0:d]).astype(BF16)
        v = dot_t(wv_t[1], xp).astype(BF16)
        for j in range(step):
            rows = slice(j * cells, (j + 1) * cells)
            kcross[base + j] = k[rows]
            put_values(vcross, base + j, pl.ds(0, cells), v[:, rows], jnp.full((1, cells), flags[j], F32))

    def cross_keys(b, p):
        return [kcross[links[comp, j, b], :, pl.ds(p * pair, pair)] for j in range(KC)]

    def cross_values(b, p):
        return jnp.concatenate([vcross[links[comp, j, b], pl.ds(p * vrows, vrows)] for j in range(KC)], axis=1)

    attend_bands(
        0, nb, pairs, pair, cross_keys, cross_values, cqbd,
        (cs0, cs1), (ce0, ce1), (m0, m1, m2, m3, m4, m5), result=cross_res,
    )

    half = cells // 2
    above, below = flag(tile > 0), flag(tile < n_tile - 1)

    def window_kv(pieces):
        flags, counts, rows = [], [], []
        for ref, at, row_flags in pieces:
            rows.append(ref[at].astype(F32).reshape(cells, d))
            flags += row_flags
            counts += [cells // len(row_flags)] * len(row_flags)
        x = scaled(jnp.concatenate(rows, axis=0))
        xa = (x * gains[0:1, :].astype(F32) * expand(flags, counts, 0)).astype(BF16)
        k, v = dot(xa, wqkv[:, d : 2 * d]).astype(BF16), dot_t(wv_t[0], xa).astype(BF16)
        return k, v

    def put_window(pieces, places, lane):
        k, v = window_kv(pieces)
        for j, ((_, _, row_flags), at) in enumerate(zip(pieces, places)):
            rows = slice(j * cells, (j + 1) * cells)
            kwin[at, pl.ds(lane, cells)] = k[rows]
            row = expand(row_flags, [cells // len(row_flags)] * len(row_flags), 1)
            put_values(vwin, at, pl.ds(lane, cells), v[:, rows], row)

    def beside(bands):
        return [(side, 1 + at, [usable(tile, left, at), usable(tile, right, at)]) for at in bands]

    for copy in edge_copies:
        copy.wait_recv()
    for copy in corner_copies:
        copy.start()
    for copy in end_copies:
        copy.wait_recv()
    put_window(
        [(ends, 0, [above * usable(up, face, nb - 1)]), (ends, 1, [below * usable(down, face, 0)])], (0, nb + 1), 0
    )

    def window_keys(lane):
        return lambda b, p: [kwin[b + j, pl.ds(lane, cells), pl.ds(p * pair, pair)] for j in range(3)]

    def window_values(lane):
        return lambda b, p: jnp.concatenate(
            [vwin[b + j, pl.ds(p * vrows, vrows), pl.ds(lane, cells)] for j in range(3)], axis=1
        )

    held = (held_values, held_totals, held_peaks)
    attend_bands(
        0, nb, pairs, pair, window_keys(0), window_values(0), qbd,
        (ws0, ws1), (we0, we1), (m0, m1, m2, m3, m4, m5), held=held,
    )

    def attend_sides(start, end):
        attend_bands(
            start, end, pairs, pair, window_keys(cells), window_values(cells), qbd,
            (ws0, ws1), (we0, we1), (m0, m1, m2, m3, m4, m5), result=win_res, held=held,
        )

    ff = wup.shape[1]
    part_ff = ff // 4

    def finish(base):
        live = expand([flag(is_air | (base + j >= own_land)) for j in range(step)], [cells] * step, 0)
        update = dot(win_res[pl.ds(base, step)].reshape(chunk, d), wout[...])
        update = update + dot(cross_res[pl.ds(base, step)].reshape(chunk, d), wcout[...])
        middle = own[pl.ds(base, step)].astype(F32).reshape(chunk, d) + live * update
        mlp_input = (scaled(middle) * gains[2:3, :].astype(F32)).astype(BF16)
        total = None
        for f in range(4):
            cols = slice(f * part_ff, (f + 1) * part_ff)
            hidden = jax.nn.silu(dot(mlp_input, wup[:, cols])).astype(BF16)
            piece = dot(hidden, wdown[cols, :])
            total = piece if total is None else total + piece
        out_ref[pl.ds(base * cells, chunk), :] = (middle + live * total).astype(BF16)

    for copy in corner_copies + near_copies:
        copy.wait_recv()
    corners = [
        (side, 0, [above * usable(up, at, nb - 1) for at in (left, right)]),
        (side, nb + 1, [below * usable(down, at, 0) for at in (left, right)]),
    ]
    bands = [0, nb - 1] + list(range(1, 1 + step // 2))
    put_window(corners + beside(bands), [0, nb + 1] + [1 + at for at in bands], cells)
    attend_sides(0, step // 2)

    for copy in mid_copies:
        copy.wait_recv()
    bands = list(range(1 + step // 2, 1 + step))
    put_window(beside(bands), [1 + at for at in bands], cells)
    attend_sides(step // 2, step)
    for copy in local[4:]:
        copy.wait()
    finish(0)

    for copy in far_copies:
        copy.wait_recv()
    bands = list(range(1 + step, nb - 1))
    put_window(beside(bands), [1 + at for at in bands], cells)
    attend_sides(step, nb)
    finish(step)

    for copy in edge_copies + near_copies + mid_copies + far_copies + end_copies + comp_copies + corner_copies:
        copy.wait_send()


def per_device(
    tokens,
    norm_gains,
    qkv_weight,
    out_weight,
    cross_query,
    cross_kv,
    cross_out,
    up_weight,
    down_weight,
    intersection_list,
    land_bands,
):
    _, rows, cols, d = tokens.shape
    nb = rows // BR
    cells = BR * cols
    groups = cells // BR
    ff = up_weight.shape[2]
    pair = 2 * (d // HEADS)
    vrows = (d // pair) * (pair + EXTRA)
    links = jnp.transpose(intersection_list, (0, 2, 3, 1)).reshape(2, KC, nb)
    smem = pl.BlockSpec(memory_space=pltpu.SMEM)
    hbm = pl.BlockSpec(memory_space=pl.ANY)
    out = pl.pallas_call(
        kernel,
        out_shape=jax.ShapeDtypeStruct((nb * cells, d), BF16),
        in_specs=[smem] * 2 + [hbm] * 10,
        out_specs=pl.BlockSpec(memory_space=pltpu.VMEM),
        scratch_shapes=[
            pltpu.VMEM((nb, groups, BR, d), BF16),
            pltpu.VMEM((nb + 2, groups, BR, d), BF16),
            pltpu.VMEM((2, groups, BR, d), BF16),
            pltpu.VMEM((nb, groups, BR, d), BF16),
            pltpu.VMEM((3, d), BF16),
            pltpu.VMEM((3, d), BF16),
            pltpu.VMEM((d, 3 * d), BF16),
            pltpu.VMEM((d, d), BF16),
            pltpu.VMEM((d, d), BF16),
            pltpu.VMEM((d, 2 * d), BF16),
            pltpu.VMEM((d, d), BF16),
            pltpu.VMEM((d, ff), BF16),
            pltpu.VMEM((ff, d), BF16),
            pltpu.VMEM((2, d, d), BF16),
            pltpu.VMEM((nb, d // pair, 2 * cells, pair), BF16),
            pltpu.VMEM((nb, d // pair, 2 * cells, pair), BF16),
            pltpu.VMEM((nb + 2, 2 * cells, d), BF16),
            pltpu.VMEM((nb + 2, vrows, 2 * cells), BF16),
            pltpu.VMEM((nb, cells, d), BF16),
            pltpu.VMEM((nb, vrows, cells), BF16),
            pltpu.VMEM((nb, cells, d), BF16),
            pltpu.VMEM((nb, cells, d), BF16),
            *[pltpu.VMEM((KC * cells, 2 * cells), F32)] * 2,
            *[pltpu.VMEM((KC * cells, 2 * cells), BF16)] * 2,
            *[pltpu.VMEM((3 * cells, 2 * cells), F32)] * 2,
            *[pltpu.VMEM((3 * cells, 2 * cells), BF16)] * 2,
            *[pltpu.VMEM((8, 2 * cells), F32)] * 6,
            pltpu.VMEM((nb, d // pair, pair // 2, 2 * cells), F32),
            pltpu.VMEM((nb, d // pair, 8, 2 * cells), F32),
            pltpu.VMEM((nb, d // pair, 8, 2 * cells), F32),
            pltpu.SemaphoreType.DMA((17,)),
            pltpu.SemaphoreType.DMA((17,)),
            pltpu.SemaphoreType.DMA((8,)),
        ],
        compiler_params=pltpu.CompilerParams(
            collective_id=0, has_side_effects=True, vmem_limit_bytes=56 * 1024 * 1024
        ),
    )(
        links,
        land_bands,
        tokens.reshape(nb, BR, cols // BR, BR, d),
        tokens.reshape(nb, groups, BR, d),
        norm_gains[0],
        qkv_weight[0],
        out_weight[0],
        cross_query[0],
        cross_kv[0],
        cross_out[0],
        up_weight[0],
        down_weight[0],
    )
    return out.reshape(1, rows, cols, d)


def solution(mesh):
    placed = (
        P("comp", "tile", "face", None),
        P("comp", None, None),
        P("comp", None, None),
        P("comp", None, None),
        P("comp", None, None),
        P("comp", None, None),
        P("comp", None, None),
        P("comp", None, None),
        P("comp", None, None),
        P(None, "tile", "face", None),
        P(),
    )
    return jax.shard_map(
        per_device,
        mesh=mesh,
        in_specs=placed,
        out_specs=P("comp", "tile", "face", None),
        check_vma=False,
    )
```

```python
import functools

import jax
import jax.numpy as jnp
from jax import lax
from jax.experimental import pallas as pl
from jax.experimental.pallas import tpu as pltpu
from jax.sharding import PartitionSpec as P

HEADS = 8
BR = 8
KC = 4
EPSILON = 1e-05
EXTRA = 16
LOG2E = 1.4426950408889634
MESH = pl.DeviceIdType.MESH
F32 = jnp.float32
BF16 = jnp.bfloat16


def dot(a, b):
    return lax.dot_general(a, b, (((1,), (0,)), ((), ())), preferred_element_type=F32)


def dot_t(a, b):
    return lax.dot_general(a, b, (((1,), (1,)), ((), ())), preferred_element_type=F32)


def attend_bands(start, end, pairs, pair, keys_of, values_of, queries, scores, terms, peaks, result=None, held=None, stride=1, hook=None):
    cells = queries.shape[2] // 2
    half = pair // 2

    def score(i, p, slot):
        b = i * stride
        q = queries[b, p]
        top = jnp.zeros((8, 2 * cells), F32)
        if result is not None and held is not None:
            top = held[2][b, p]
        row = 0
        for keys in keys_of(b, p):
            rows = keys.shape[0]
            s = dot_t(keys, q)
            scores[slot][pl.ds(row, rows), :] = s
            top = jnp.maximum(top, jnp.max(s.reshape(rows // 8, 8, 2 * cells), axis=0))
            row += rows
        peaks[slot][...] = jnp.broadcast_to(jnp.max(top, axis=0, keepdims=True), (8, 2 * cells))

    def blend(i, p, slot):
        b = i * stride
        blended = dot(values_of(b, p), terms[slot][...])
        first, second = blended[:half, :cells], blended[half:pair, cells:]
        total = blended[pair : pair + 8, :]
        if result is None:
            held[0][b, p, :, pl.ds(0, cells)] = first
            held[0][b, p, :, pl.ds(cells, cells)] = second
            held[1][b, p] = total
            return
        total = total[0:1, :] + peaks[2 + slot][0:1, :]
        if held is not None:
            fade = peaks[4 + slot][0:1, :]
            total = total + held[1][b, p, 0:1, :] * fade
            first = first + held[0][b, p, :, pl.ds(0, cells)] * fade[:, :cells]
            second = second + held[0][b, p, :, pl.ds(cells, cells)] * fade[:, cells:]
        inverse = 1.0 / total
        first = first * inverse[:, :cells]
        second = second * inverse[:, cells:]
        result[b, :, pl.ds(p * pair, pair)] = jnp.concatenate([first, second], axis=0).T.astype(BF16)

    def weigh(i, p, slot):
        b = i * stride
        peak = peaks[slot][0:1, :]
        terms[slot][...] = jnp.exp2(scores[slot][...] - peak).astype(BF16)
        if result is None:
            held[2][b, p] = peaks[slot][...]
            return
        peaks[2 + slot][...] = jnp.exp2(-peaks[slot][...])
        if held is not None:
            peaks[4 + slot][...] = jnp.exp2(held[2][b, p] - peaks[slot][...])

    last = (pairs - 1) % 2
    terms[last][...] = jnp.zeros(terms[last].shape, BF16)
    peaks[2 + last][...] = jnp.ones(peaks[2 + last].shape, F32)
    peaks[4 + last][...] = jnp.ones(peaks[4 + last].shape, F32)
    score(start, 0, 0)

    @pl.loop(start, end)
    def _(b):
        if hook is not None:
            hook(b)
        for p in range(pairs):
            slot = p % 2
            if p + 1 < pairs:
                score(b, p + 1, 1 - slot)
            else:
                score(jnp.minimum(b + 1, end - 1), 0, 1 - slot)
            if p > 0:
                blend(b, p - 1, 1 - slot)
            else:
                blend(jnp.maximum(b - 1, start), pairs - 1, 1 - slot)
            weigh(b, p, slot)

    blend(end - 1, pairs - 1, last)


def kernel(
    links,
    land,
    tok5,
    tok4,
    gains_hbm,
    wqkv_hbm,
    wout_hbm,
    wcq_hbm,
    wckv_hbm,
    wcout_hbm,
    wup_hbm,
    wdown_hbm,
    out_ref,
    own,
    side,
    ends,
    part,
    gains,
    gains_p,
    wqkv,
    wout,
    wcq,
    wckv,
    wcout,
    wup,
    wdown,
    wv_t,
    qbd,
    cqbd,
    kwin,
    vwin,
    kcross,
    vcross,
    win_res,
    cross_res,
    cs0,
    cs1,
    ce0,
    ce1,
    ws0,
    ws1,
    we0,
    we1,
    out_all,
    m0,
    m1,
    m2,
    m3,
    m4,
    m5,
    held_values,
    held_totals,
    held_peaks,
    send_sem,
    recv_sem,
    local_sem,
    out_sem,
):
    nb, groups, _, d = own.shape
    cells = groups * BR
    pair = 2 * (d // HEADS)
    pairs = d // pair
    vrows = pair + EXTRA
    comp, face, tile = (lax.axis_index(a) for a in ("comp", "face", "tile"))
    n_face, n_tile = lax.axis_size("face"), lax.axis_size("tile")
    left, right = lax.rem(face + n_face - 1, n_face), lax.rem(face + 1, n_face)
    up, down = lax.rem(tile + n_tile - 1, n_tile), lax.rem(tile + 1, n_tile)
    other = 1 - comp

    local = [
        pltpu.make_async_copy(src, dst, local_sem.at[i])
        for i, (src, dst) in enumerate(
            (
                (tok4, own),
                (gains_hbm, gains),
                (wqkv_hbm, wqkv),
                (wcq_hbm, wcq),
                (wcout_hbm, wcout),
                (wout_hbm, wout),
                (wup_hbm, wup),
                (wdown_hbm, wdown),
            )
        )
    ]
    for copy in local[:4]:
        copy.start()

    barrier = pltpu.get_barrier_semaphore()
    for target in ({"comp": other}, {"face": left}, {"face": right}, {"tile": up}, {"tile": down}):
        pl.semaphore_signal(barrier, inc=1, device_id=target, device_id_type=MESH)

    def remote(i, src, dst, target):
        return pltpu.make_async_remote_copy(
            src_ref=src,
            dst_ref=dst,
            send_sem=send_sem.at[i],
            recv_sem=recv_sem.at[i],
            device_id=target,
            device_id_type=MESH,
        )

    def to_face(i, first, count):
        bands = pl.ds(first, count)
        return [
            remote(i, tok5.at[bands, :, 0], side.at[pl.ds(1 + first, count), pl.ds(BR, BR)], {"face": left}),
            remote(i + 1, tok5.at[bands, :, 1], side.at[pl.ds(1 + first, count), pl.ds(0, BR)], {"face": right}),
        ]

    edge_copies = to_face(0, 0, 1) + to_face(2, nb - 1, 1)
    step = nb // 2
    near_copies = to_face(4, 1, step // 2)
    mid_copies = to_face(15, 1 + step // 2, step - step // 2)
    far_copies = to_face(13, 1 + step, nb - 2 - step)
    end_copies = [
        remote(6, tok4.at[0], ends.at[1], {"tile": up}),
        remote(7, tok4.at[nb - 1], ends.at[0], {"tile": down}),
    ]
    comp_copies = [
        remote(9, wckv_hbm, wckv, {"comp": other}),
        remote(10, gains_hbm, gains_p, {"comp": other}),
    ]

    def part_copy(c):
        bands = pl.ds(c * step, step)
        return remote(17 + c, tok4.at[bands], part.at[bands], {"comp": other})

    part_copies = [part_copy(c) for c in range(nb // step)]
    corner_copies = [
        remote(11, side.at[1], side.at[nb + 1], {"tile": up}),
        remote(12, side.at[nb], side.at[0], {"tile": down}),
    ]

    has_up, has_down = tile > 0, tile < n_tile - 1

    def along_tile(copies, action):
        upward, downward = copies
        first, second = (has_down, has_up) if action == "wait_recv" else (has_up, has_down)
        pl.when(first)(getattr(upward, action))
        pl.when(second)(getattr(downward, action))

    @pl.when(jnp.logical_not(has_up))
    def _():
        ends[0] = jnp.zeros(ends.shape[1:], BF16)
        side[0] = jnp.zeros(side.shape[1:], BF16)

    @pl.when(jnp.logical_not(has_down))
    def _():
        ends[1] = jnp.zeros(ends.shape[1:], BF16)
        side[nb + 1] = jnp.zeros(side.shape[1:], BF16)

    is_air = comp == 0
    own_land = land[tile, face]

    def flag(cond):
        return jnp.where(cond, 1.0, 0.0).astype(F32)

    def usable(tile_at, face_at, band):
        return flag(is_air | (band >= land[tile_at, face_at]))

    def scaled(x):
        mean_square = jnp.mean(x * x, axis=-1, keepdims=True)
        return x * lax.rsqrt(mean_square + EPSILON)

    def expand(flags, counts, axis):
        shape = (sum(counts), 1) if axis == 0 else (1, sum(counts))
        at = lax.broadcasted_iota(jnp.int32, shape, axis)
        mask = jnp.full(shape, flags[0], F32)
        start = 0
        for value, count in zip(flags[1:], counts[:-1]):
            start += count
            mask = jnp.where(at >= start, value, mask)
        return mask

    def put_values(ref, at, lanes, vals, mask_row):
        width = vals.shape[1]
        extra = jnp.broadcast_to(mask_row, (EXTRA, width)).astype(BF16)
        for p in range(pairs):
            ref[at, pl.ds(p * vrows, pair), lanes] = vals[p * pair : (p + 1) * pair, :]
            ref[at, pl.ds(p * vrows + pair, EXTRA), lanes] = extra

    def put_queries(ref, b, q):
        lane = lax.broadcasted_iota(jnp.int32, (1, d), 1)
        low = lax.rem(lane, pair) < pair // 2
        q = q * float((d // HEADS) ** -0.5 * LOG2E)
        q_low = jnp.where(low, q, 0.0).astype(BF16)
        q_high = jnp.where(low, 0.0, q).astype(BF16)
        for p in range(pairs):
            ref[b, p, pl.ds(0, cells)] = q_low[:, p * pair : (p + 1) * pair]
            ref[b, p, pl.ds(cells, cells)] = q_high[:, p * pair : (p + 1) * pair]

    for copy in local[:4]:
        copy.wait()
    wv_t[0] = wqkv[:, 2 * d : 3 * d].T
    chunk = step * cells

    @pl.loop(0, nb // step)
    def _(c):
        @pl.when(c == nb // step - 1)
        def _():
            pl.semaphore_wait(barrier, 5)
            for copy in comp_copies + part_copies[:1] + edge_copies + part_copies[1:]:
                copy.start()
            along_tile(end_copies, "start")
            for copy in near_copies:
                copy.start()
            for copy in local[4:]:
                copy.start()

        base = c * step
        x = own[pl.ds(base, step)].astype(F32).reshape(chunk, d)
        x = scaled(x)
        flags = [usable(tile, face, base + j) for j in range(step)]
        xa = (x * gains[0:1, :].astype(F32) * expand(flags, [cells] * step, 0)).astype(BF16)
        xc = (x * gains[1:2, :].astype(F32)).astype(BF16)
        q = dot(xa, wqkv[:, 0:d])
        cq = dot(xc, wcq[...])
        k = dot(xa, wqkv[:, d : 2 * d]).astype(BF16)
        v = dot_t(wv_t[0], xa).astype(BF16)
        for j in range(step):
            rows = slice(j * cells, (j + 1) * cells)
            put_queries(qbd, base + j, q[rows])
            put_queries(cqbd, base + j, cq[rows])
            kwin[1 + base + j, pl.ds(0, cells)] = k[rows]
            put_values(vwin, 1 + base + j, pl.ds(0, cells), v[:, rows], jnp.full((1, cells), flags[j], F32))


    def window_keys(lane):
        return lambda b, p: [kwin[b + j, pl.ds(lane, cells), pl.ds(p * pair, pair)] for j in range(3)]

    def window_values(lane):
        return lambda b, p: jnp.concatenate(
            [vwin[b + j, pl.ds(p * vrows, vrows), pl.ds(lane, cells)] for j in range(3)], axis=1
        )

    held = (held_values, held_totals, held_peaks)
    attend_bands(
        1, nb - 1, pairs, pair, window_keys(0), window_values(0), qbd,
        (ws0, ws1), (we0, we1), (m0, m1, m2, m3, m4, m5), held=held,
    )

    for copy in comp_copies:
        copy.wait_recv()
    wv_t[1] = wckv[:, d : 2 * d].T

    @pl.loop(0, nb // step)
    def _(c):
        base = c * step
        part_copy(c).wait_recv()
        x = scaled(part[pl.ds(base, step)].astype(F32).reshape(chunk, d))
        flags = [flag((comp == 1) | (base + j >= own_land)) for j in range(step)]
        xp = (x * gains_p[1:2, :].astype(F32) * expand(flags, [cells] * step, 0)).astype(BF16)
        k = dot(xp, wckv[:, 0:d]).astype(BF16)
        v = dot_t(wv_t[1], xp).astype(BF16)
        for j in range(step):
            rows = slice(j * cells, (j + 1) * cells)
            kcross[base + j] = k[rows]
            put_values(vcross, base + j, pl.ds(0, cells), v[:, rows], jnp.full((1, cells), flags[j], F32))

    def cross_keys(b, p):
        return [kcross[links[comp, j, b], :, pl.ds(p * pair, pair)] for j in range(KC)]

    def cross_values(b, p):
        return jnp.concatenate([vcross[links[comp, j, b], pl.ds(p * vrows, vrows)] for j in range(KC)], axis=1)

    def relay(b):
        @pl.when(b == nb // 2)
        def _():
            for copy in edge_copies:
                copy.wait_recv()
            along_tile(corner_copies, "start")
            for copy in mid_copies + far_copies:
                copy.start()

    attend_bands(
        0, nb, pairs, pair, cross_keys, cross_values, cqbd,
        (cs0, cs1), (ce0, ce1), (m0, m1, m2, m3, m4, m5), result=cross_res, hook=relay,
    )

    half = cells // 2
    above, below = flag(tile > 0), flag(tile < n_tile - 1)

    def window_kv(pieces):
        flags, counts, rows = [], [], []
        for ref, at, row_flags in pieces:
            rows.append(ref[at].astype(F32).reshape(cells, d))
            flags += row_flags
            counts += [cells // len(row_flags)] * len(row_flags)
        x = scaled(jnp.concatenate(rows, axis=0))
        xa = (x * gains[0:1, :].astype(F32) * expand(flags, counts, 0)).astype(BF16)
        k, v = dot(xa, wqkv[:, d : 2 * d]).astype(BF16), dot_t(wv_t[0], xa).astype(BF16)
        return k, v

    def put_window(pieces, places, lane):
        k, v = window_kv(pieces)
        for j, ((_, _, row_flags), at) in enumerate(zip(pieces, places)):
            rows = slice(j * cells, (j + 1) * cells)
            kwin[at, pl.ds(lane, cells)] = k[rows]
            row = expand(row_flags, [cells // len(row_flags)] * len(row_flags), 1)
            put_values(vwin, at, pl.ds(lane, cells), v[:, rows], row)

    def beside(bands):
        return [(side, 1 + at, [usable(tile, left, at), usable(tile, right, at)]) for at in bands]

    along_tile(end_copies, "wait_recv")
    put_window(
        [(ends, 0, [above * usable(up, face, nb - 1)]), (ends, 1, [below * usable(down, face, 0)])], (0, nb + 1), 0
    )

    attend_bands(
        0, 2, pairs, pair, window_keys(0), window_values(0), qbd,
        (ws0, ws1), (we0, we1), (m0, m1, m2, m3, m4, m5), held=held, stride=nb - 1,
    )

    def attend_sides(start, end):
        attend_bands(
            start, end, pairs, pair, window_keys(cells), window_values(cells), qbd,
            (ws0, ws1), (we0, we1), (m0, m1, m2, m3, m4, m5), result=win_res, held=held,
        )

    ff = wup.shape[1]
    part_ff = ff // 4

    def out_copy(base, j):
        at = pl.ds(base * cells + j * (chunk // 2), chunk // 2)
        i = 2 * (base // step) + j
        return pltpu.make_async_copy(out_all.at[at], out_ref.at[at], out_sem.at[i])

    def finish(base):
        live = expand([flag(is_air | (base + j >= own_land)) for j in range(step)], [cells] * step, 0)
        update = dot(win_res[pl.ds(base, step)].reshape(chunk, d), wout[...])
        update = update + dot(cross_res[pl.ds(base, step)].reshape(chunk, d), wcout[...])
        middle = own[pl.ds(base, step)].astype(F32).reshape(chunk, d) + live * update
        mlp_input = (scaled(middle) * gains[2:3, :].astype(F32)).astype(BF16)
        total = None
        for f in range(3):
            cols = slice(f * part_ff, (f + 1) * part_ff)
            hidden = jax.nn.silu(dot(mlp_input, wup[:, cols])).astype(BF16)
            piece = dot(hidden, wdown[cols, :])
            total = piece if total is None else total + piece
        cols = slice(3 * part_ff, ff)
        hidden = jax.nn.silu(dot(mlp_input, wup[:, cols])).astype(BF16)
        for j in range(2):
            rows = slice(j * chunk // 2, (j + 1) * chunk // 2)
            piece = total[rows] + dot(hidden[rows], wdown[cols, :])
            at = pl.ds(base * cells + j * (chunk // 2), chunk // 2)
            out_all[at, :] = (middle[rows] + live[rows] * piece).astype(BF16)
            out_copy(base, j).start()

    along_tile(corner_copies, "wait_recv")
    for copy in near_copies:
        copy.wait_recv()
    corners = [
        (side, 0, [above * usable(up, at, nb - 1) for at in (left, right)]),
        (side, nb + 1, [below * usable(down, at, 0) for at in (left, right)]),
    ]
    bands = [0, nb - 1] + list(range(1, 1 + step // 2))
    put_window(corners + beside(bands), [0, nb + 1] + [1 + at for at in bands], cells)
    attend_sides(0, step // 2)

    for copy in mid_copies:
        copy.wait_recv()
    bands = list(range(1 + step // 2, 1 + step))
    put_window(beside(bands), [1 + at for at in bands], cells)
    attend_sides(step // 2, step)
    for copy in local[4:]:
        copy.wait()
    finish(0)

    for copy in far_copies:
        copy.wait_recv()
    bands = list(range(1 + step, nb - 1))
    put_window(beside(bands), [1 + at for at in bands], cells)
    attend_sides(step, nb)
    finish(step)

    for copy in edge_copies + near_copies + mid_copies + far_copies + comp_copies + part_copies:
        copy.wait_send()
    along_tile(end_copies, "wait_send")
    along_tile(corner_copies, "wait_send")
    for base in range(0, nb, step):
        for j in range(2):
            out_copy(base, j).wait()


def per_device(
    tokens,
    norm_gains,
    qkv_weight,
    out_weight,
    cross_query,
    cross_kv,
    cross_out,
    up_weight,
    down_weight,
    intersection_list,
    land_bands,
):
    _, rows, cols, d = tokens.shape
    nb = rows // BR
    cells = BR * cols
    groups = cells // BR
    ff = up_weight.shape[2]
    pair = 2 * (d // HEADS)
    vrows = (d // pair) * (pair + EXTRA)
    links = jnp.transpose(intersection_list, (0, 2, 3, 1)).reshape(2, KC, nb)
    smem = pl.BlockSpec(memory_space=pltpu.SMEM)
    hbm = pl.BlockSpec(memory_space=pl.ANY)
    out = pl.pallas_call(
        kernel,
        out_shape=jax.ShapeDtypeStruct((nb * cells, d), BF16),
        in_specs=[smem] * 2 + [hbm] * 10,
        out_specs=hbm,
        scratch_shapes=[
            pltpu.VMEM((nb, groups, BR, d), BF16),
            pltpu.VMEM((nb + 2, groups, BR, d), BF16),
            pltpu.VMEM((2, groups, BR, d), BF16),
            pltpu.VMEM((nb, groups, BR, d), BF16),
            pltpu.VMEM((3, d), BF16),
            pltpu.VMEM((3, d), BF16),
            pltpu.VMEM((d, 3 * d), BF16),
            pltpu.VMEM((d, d), BF16),
            pltpu.VMEM((d, d), BF16),
            pltpu.VMEM((d, 2 * d), BF16),
            pltpu.VMEM((d, d), BF16),
            pltpu.VMEM((d, ff), BF16),
            pltpu.VMEM((ff, d), BF16),
            pltpu.VMEM((2, d, d), BF16),
            pltpu.VMEM((nb, d // pair, 2 * cells, pair), BF16),
            pltpu.VMEM((nb, d // pair, 2 * cells, pair), BF16),
            pltpu.VMEM((nb + 2, 2 * cells, d), BF16),
            pltpu.VMEM((nb + 2, vrows, 2 * cells), BF16),
            pltpu.VMEM((nb, cells, d), BF16),
            pltpu.VMEM((nb, vrows, cells), BF16),
            pltpu.VMEM((nb, cells, d), BF16),
            pltpu.VMEM((nb, cells, d), BF16),
            *[pltpu.VMEM((KC * cells, 2 * cells), F32)] * 2,
            *[pltpu.VMEM((KC * cells, 2 * cells), BF16)] * 2,
            *[pltpu.VMEM((3 * cells, 2 * cells), F32)] * 2,
            *[pltpu.VMEM((3 * cells, 2 * cells), BF16)] * 2,
            pltpu.VMEM((nb * cells, d), BF16),
            *[pltpu.VMEM((8, 2 * cells), F32)] * 6,
            pltpu.VMEM((nb, d // pair, pair // 2, 2 * cells), F32),
            pltpu.VMEM((nb, d // pair, 8, 2 * cells), F32),
            pltpu.VMEM((nb, d // pair, 8, 2 * cells), F32),
            pltpu.SemaphoreType.DMA((19,)),
            pltpu.SemaphoreType.DMA((19,)),
            pltpu.SemaphoreType.DMA((8,)),
            pltpu.SemaphoreType.DMA((2 * nb // (nb // 2),)),
        ],
        compiler_params=pltpu.CompilerParams(
            collective_id=0, has_side_effects=True, vmem_limit_bytes=56 * 1024 * 1024
        ),
    )(
        links,
        land_bands,
        tokens.reshape(nb, BR, cols // BR, BR, d),
        tokens.reshape(nb, groups, BR, d),
        norm_gains[0],
        qkv_weight[0],
        out_weight[0],
        cross_query[0],
        cross_kv[0],
        cross_out[0],
        up_weight[0],
        down_weight[0],
    )
    return out.reshape(1, rows, cols, d)


def solution(mesh):
    placed = (
        P("comp", "tile", "face", None),
        P("comp", None, None),
        P("comp", None, None),
        P("comp", None, None),
        P("comp", None, None),
        P("comp", None, None),
        P("comp", None, None),
        P("comp", None, None),
        P("comp", None, None),
        P(None, "tile", "face", None),
        P(),
    )
    return jax.shard_map(
        per_device,
        mesh=mesh,
        in_specs=placed,
        out_specs=P("comp", "tile", "face", None),
        check_vma=False,
    )
```
